512 devices in a mesh: seq: 64 (over z, y_lo, core), head: 8 (over x, y_hi).
Axes of the slice: x: 4, y: 4 (y_hi: 2, y_lo: 2; y = y_hi * 2 + y_lo), z: 16, core: 2. Of those that a mesh axis runs over, the one named last changes fastest.
Arguments:
- queries: bfloat16 [4096, 3072], P('seq', 'head'), may hold values from -10 to 10
- suffix_latent: bfloat16 [4096, 576], P('seq'), may hold values from -6 to 6
- prefix_latent: bfloat16 [1024, 576], P('seq'), may hold values from -6 to 6
- kv_up: bfloat16 [16, 512, 256], P('head'), may hold values from -0.25 to 0.25
- w_out: bfloat16 [2048, 2048], P('head'), may hold values from -2 to 2
- residual: bfloat16 [4096, 2048], P('seq'), may hold values from -400 to 400
- norm_gain: bfloat16 [2048], replicated, may hold values from 0.099609375 to 1.8984375
- router: bfloat16 [2048, 64], replicated, may hold values from -0.125 to 0.125
- w_gate: bfloat16 [64, 2048, 1408], P('seq', None, 'head'), may hold values from -0.125 to 0.125
- w_up: bfloat16 [64, 2048, 1408], P('seq', None, 'head'), may hold values from -0.125 to 0.125
- w_down: bfloat16 [64, 1408, 2048], P('seq', 'head'), may hold values from -0.15625 to 0.15625
- lengths: int32 [128], replicated, may hold values from 1 to 64, 4096 in all
- group_map: int32 [128], replicated, may hold values from 0 to 1
- expert_ids: int32 [4096, 6], P('seq'), may hold values from 0 to 63, all different within a row; in each aligned block of 64 rows (0 to 63, 64 to 127, ...) at most 9 rows name the same one
Outputs:
- attention: bfloat16 [4096, 2048], P('seq', 'head')
- expert_out: bfloat16 [4096, 2048], P('seq', 'head')
The draws below stay inside these ranges and needn't reach their ends.
Inputs may be any that keep to these rules, and one draw needn't show every extreme that they name: `lengths`: the requests cover the 4096 tokens exactly; each has 1 to 64 tokens, and one has exactly 64. `expert_ids`: each token names 6 different experts. Among the 64 tokens of one index of seq (aligned blocks of rows) no expert is named more than 9 times, a bound that some block reaches.
All inputs are finite; a program needn't handle non-finite values.
Results may differ from the reference program's by a relative error of at most 0.027.
Values may be sent and summed in bfloat16 or wider, within the bound.
A program may use at most 64 MiB of HBM per device.

```python
import math
import jax
import jax.numpy as jnp
import numpy as np
from jax import lax

D = 2048
HEADS = 16
NOPE = 128
ROPE = 64
VDIM = 128
LAT = 512
FF = 1408
TOPK = 6
TOK_DEV = 64
GROUPS = 2
PRE_LEN = 512
EXPERTS = 64
TOKENS = 4096
REQUESTS = 128
PREFIX = 1024
CAP = 9
FF_PART = 176
N_SEQ = 64


def draw_queries(key, part):
    base = jnp.clip(jax.random.normal(jax.random.fold_in(key, 3), (TOKENS, HEADS, NOPE + ROPE), jnp.float32), -6.0, 6.0)
    return base.reshape(TOKENS, HEADS * (NOPE + ROPE)).astype(jnp.bfloat16)


def draw_suffix_latent(key, part):
    base = jnp.clip(jax.random.normal(jax.random.fold_in(key, 5), (TOKENS, LAT + ROPE), jnp.float32), -6.0, 6.0)
    return base.astype(jnp.bfloat16)


def draw_residual(key, part):
    noise = jnp.clip(jax.random.normal(jax.random.fold_in(key, 1), (TOKENS, D), jnp.float32), -4.0, 4.0)
    row_scale = jnp.exp(jax.random.uniform(jax.random.fold_in(key, 2), (TOKENS, 1), jnp.float32) * math.log(10.0))
    col_scale = jnp.exp(jax.random.uniform(jax.random.fold_in(key, 4), (1, D), jnp.float32) * math.log(10.0))
    return (noise * row_scale * col_scale).astype(jnp.bfloat16)


def place_ends(drawn, rng, least, high):
    shape = drawn.shape
    place = [jax.random.randint(jax.random.fold_in(rng, axis), (), 0, shape[axis]) for axis in range(len(shape))]
    drawn = drawn.at[tuple(place)].set(least)
    longest = shape.index(max(shape))
    place[longest] = (place[longest] + 1) % shape[longest]
    return drawn.at[tuple(place)].set(high)


def block_scale(key, extent, shards, least, high):
    level = 1.0
    for dim, blocks in shards:
        draws = jax.random.uniform(jax.random.fold_in(jax.random.fold_in(key, 6), dim), (blocks,), jnp.float32, least / len(shards), high / len(shards))
        level = level * jnp.repeat(jnp.exp(draws), extent[dim] // blocks).reshape((-1,) + (1,) * (len(extent) - 1 - dim))
    return level


def length_profile(amount, total, bound, slope):
    weights = [(1 << 20) // math.isqrt(rank ** slope) + 1 for rank in range(2, amount + 1)]
    spare, holding = total - bound - (amount - 1), [1] * (amount - 1)
    while spare > 0:
        movable = [i for i in range(amount - 1) if holding[i] < bound]
        pool, left = sum([weights[i] for i in movable]), spare
        for i in movable:
            more = min(bound - holding[i], max(1, left * weights[i] // pool), spare)
            holding[i] = holding[i] + more
            spare = spare - more
    return np.array([bound] + holding)


def ragged(stream_key, amount, total, limit, slope):
    if amount == 2:
        one = jax.random.randint(stream_key, (), max(1, total - limit), min(limit, total - 1) + 1)
        return jnp.stack([one, total - one])
    sizes = jnp.asarray(length_profile(amount, total, limit, slope), jnp.int32)
    twos = (amount - 1) // 2
    donor, sink = sizes[1:1 + 2 * twos:2], sizes[2:2 + 2 * twos:2]
    room = jnp.minimum(donor - 1, limit - sink)
    passed = jax.random.randint(jax.random.fold_in(stream_key, 1), (twos,), 0, 1 << 20) % (room + 1)
    sizes = sizes.at[1:1 + 2 * twos:2].set(donor - passed).at[2:2 + 2 * twos:2].set(sink + passed)
    return sizes[jax.random.permutation(jax.random.fold_in(stream_key, 2), amount)]


def deal_out(own_key, own, number, rows, number_of, top, most, lean):
    sequence = jax.random.permutation(own_key, number_of)
    heavy_load, ordinary = portions_of(number_of, rows * top, most, lean, True), portions_of(number_of, rows * top, most, lean, False)
    places = jnp.arange(number_of)

    def named(tallies, rotation):
        used = int((tallies > 0).sum())
        fixed = max(1, used // 4)
        passed = fixed + (places - fixed + rotation * (used - fixed)) % max(1, number_of - fixed)
        return jnp.zeros((number_of,), jnp.int32).at[sequence[jnp.where(places < fixed, places, passed)]].set(jnp.asarray(tallies, jnp.int32))

    tallies = jnp.where(number % 4 == 0, named(heavy_load, number // 4), named(ordinary, number - number // 4 - 1))
    mixed = jax.random.permutation(jax.random.fold_in(own, 3), number_of)
    donor, sink = mixed[0:number_of // 2 * 2:2], mixed[1:number_of // 2 * 2:2]
    slack = jnp.minimum(tallies[donor] - 1, most - tallies[sink]) // 2
    slack = jnp.where((donor == sequence[0]) | (sink == sequence[0]) | (tallies[sink] == 0), 0, jnp.maximum(slack, 0))
    passed = jax.random.randint(jax.random.fold_in(own, 4), (number_of // 2,), 0, 1 << 20) % (slack + 1)
    tallies = tallies.at[donor].add(-passed).at[sink].add(passed)
    members = jnp.searchsorted(jnp.cumsum(tallies), jnp.arange(rows * top), side="right").astype(jnp.int32)
    grid = members.reshape(top, rows).T
    grid = grid[jax.random.permutation(jax.random.fold_in(own, 1), rows)]
    rotation = jax.random.randint(jax.random.fold_in(own, 2), (rows, 1), 0, top)
    return jnp.take_along_axis(grid, (jnp.arange(top)[None, :] + rotation) % top, axis=1)


def portions_of(count, total, limit, skew, full):
    weights = [(1 << 20) // math.isqrt(rank ** skew) + 1 for rank in range(1, count + 1)]
    largest = limit if full else min(limit, max(-(-total // count), total * weights[0] // sum(weights)))
    least = 1 if total - largest >= count - 1 else 0
    holding, rest = [largest] + [least] * (count - 1), total - largest - least * (count - 1)
    while rest > 0:
        free = [i for i in range(1, count) if holding[i] < largest] or [i for i in range(1, count) if holding[i] < limit]
        whole, remaining = sum([weights[i] for i in free]), rest
        for i in free:
            extra = min(limit - holding[i], max(1, remaining * weights[i] // whole), rest)
            holding[i] = holding[i] + extra
            rest = rest - extra
    return np.array(holding)


def scatter_about(own_key, dims, width, most, cuts=(), kind=jnp.bfloat16):
    factor_of = block_scale(own_key, dims, cuts, -0.22, 0.18) if cuts else 1.0
    array = jax.random.normal(own_key, dims, jnp.float32) * width * factor_of
    return jnp.minimum(jnp.maximum(array, -most), most).astype(kind)


def setup_inputs(seed: int = 0) -> dict:
    key_list = jax.random.split(jax.random.key(seed), 15)
    queries = draw_queries(jax.random.fold_in(key_list[14], 71), 0)
    suffix_latent = draw_suffix_latent(jax.random.fold_in(key_list[14], 71), 0)
    prefix_latent = scatter_about(key_list[2], (PREFIX, LAT + ROPE), 1.0, 6.0, ((0, 64),))
    kv_up = scatter_about(key_list[3], (HEADS, LAT, NOPE + VDIM), LAT ** -0.5, 0.25, ((0, 8),))
    w_out = scatter_about(key_list[4], (HEADS * VDIM, D), (max(1, HEADS * VDIM // 256)) ** -0.5, 2.0, ((0, 8),))
    residual = draw_residual(jax.random.fold_in(key_list[14], 71), 0)
    norm_gain = jnp.clip(1.0 + 0.18 * jax.random.normal(key_list[6], (D,), jnp.float32), 0.099609375, 1.8984375).astype(jnp.bfloat16)
    router = scatter_about(key_list[7], (D, EXPERTS), D ** -0.5, 0.125)
    w_gate = scatter_about(key_list[8], (EXPERTS, D, FF), D ** -0.5, 0.125, ((0, 64), (2, 8)))
    w_up = scatter_about(key_list[9], (EXPERTS, D, FF), D ** -0.5, 0.125, ((0, 64), (2, 8)))
    w_down = scatter_about(key_list[10], (EXPERTS, FF, D), FF ** -0.5, 0.15625, ((0, 64), (1, 8)))
    lengths = ragged(key_list[11], REQUESTS, TOKENS, TOK_DEV, 2).astype(jnp.int32)
    group_map = place_ends(jax.random.randint(key_list[12], (REQUESTS,), 0, GROUPS), jax.random.fold_in(key_list[12], 1), 0, GROUPS - 1).astype(jnp.int32)
    expert_ids_keys = jax.random.split(jax.random.fold_in(key_list[13], 1), TOKENS // TOK_DEV)
    expert_ids_turns = jax.random.permutation(jax.random.fold_in(key_list[13], 3), TOKENS // TOK_DEV)
    expert_ids = jax.vmap(lambda own, number: deal_out(jax.random.fold_in(key_list[13], 2), own, number, TOK_DEV, EXPERTS, TOPK, CAP, 2))(expert_ids_keys, expert_ids_turns).reshape((TOKENS, TOPK))
    return {"queries": queries, "suffix_latent": suffix_latent, "prefix_latent": prefix_latent, "kv_up": kv_up, "w_out": w_out, "residual": residual, "norm_gain": norm_gain, "router": router, "w_gate": w_gate, "w_up": w_up, "w_down": w_down, "lengths": lengths, "group_map": group_map, "expert_ids": expert_ids}


score_scale = 1.0 / math.sqrt(192.0)
route_scale = 2.446
norm_eps = 1e-06

def request_info(lengths, group_map, position):
    request_ends = jnp.cumsum(lengths).astype(jnp.int32)
    request_starts = request_ends - lengths
    request_index = lax.optimization_barrier(jnp.sum((request_ends[None, :] <= position[:, None]).astype(jnp.int32), axis=1))
    member = (request_index[:, None] == jnp.arange(lengths.shape[0], dtype=jnp.int32)[None, :]).astype(jnp.int32)
    first_token = lax.optimization_barrier(jnp.sum(member * request_starts[None, :], axis=1))
    token_group = lax.optimization_barrier(jnp.sum(member * group_map[None, :], axis=1))
    return (first_token, token_group)

def reference(queries, suffix_latent, prefix_latent, kv_up, w_out, residual, norm_gain, router, w_gate, w_up, w_down, lengths, group_map, expert_ids):
    padded = jnp.concatenate([jnp.zeros((TOK_DEV, LAT + ROPE), suffix_latent.dtype), suffix_latent], axis=0)
    prefix_group = jnp.arange(PREFIX, dtype=jnp.int32) // PRE_LEN
    key_up = kv_up[:, :, :NOPE].astype(jnp.float32)
    value_up = kv_up[:, :, NOPE:].astype(jnp.float32)

    def block_attention(block_index):
        start_row = (block_index * TOK_DEV).astype(jnp.int32)
        query_block = lax.dynamic_slice_in_dim(queries, start_row, TOK_DEV, 0).reshape(TOK_DEV, HEADS, NOPE + ROPE)
        absorbed = jnp.einsum('thn,hln->thl', query_block[:, :, :NOPE].astype(jnp.float32), key_up).astype(jnp.bfloat16)
        joined = jnp.concatenate([absorbed, query_block[:, :, NOPE:]], axis=2).reshape(TOK_DEV * HEADS, LAT + ROPE)
        nearby = lax.dynamic_slice_in_dim(padded, start_row, 2 * TOK_DEV, 0)
        all_keys = jnp.concatenate([prefix_latent, nearby], axis=0)
        scores = jnp.dot(joined, all_keys.T, preferred_element_type=jnp.float32) * score_scale
        position = start_row + jnp.arange(TOK_DEV, dtype=jnp.int32)
        first_token, token_group = request_info(lengths, group_map, position)
        near_pos = start_row - TOK_DEV + jnp.arange(2 * TOK_DEV, dtype=jnp.int32)
        near_seen = (near_pos[None, :] >= first_token[:, None]) & (near_pos[None, :] <= position[:, None])
        far_seen = prefix_group[None, :] == token_group[:, None]
        visible = jnp.repeat(jnp.concatenate([far_seen, near_seen], axis=1), HEADS, axis=0)
        row_max = lax.optimization_barrier(jnp.max(jnp.where(visible, scores, -jnp.inf), axis=1, keepdims=True))
        weights = jnp.where(visible, jnp.exp(scores - row_max), 0.0)
        total = lax.optimization_barrier(jnp.sum(weights, axis=1, keepdims=True))
        mixed = jnp.dot(weights.astype(jnp.bfloat16), all_keys[:, :LAT], preferred_element_type=jnp.float32) / total
        mixed = mixed.astype(jnp.bfloat16).reshape(TOK_DEV, HEADS, LAT)
        heads_out = jnp.einsum('thl,hlv->thv', mixed.astype(jnp.float32), value_up).astype(jnp.bfloat16)
        return jnp.dot(heads_out.reshape(TOK_DEV, HEADS * VDIM), w_out, preferred_element_type=jnp.float32)
    attention_sum = lax.map(block_attention, jnp.arange(N_SEQ, dtype=jnp.int32)).reshape(TOKENS, D)
    attention = attention_sum.astype(jnp.bfloat16)
    hidden_state = residual.astype(jnp.float32) + attention_sum
    mean_square = lax.optimization_barrier(jnp.mean(hidden_state * hidden_state, axis=1, keepdims=True))
    normed = (hidden_state * lax.rsqrt(mean_square + norm_eps) * norm_gain.astype(jnp.float32)).astype(jnp.bfloat16)
    logits = jnp.dot(normed, router, preferred_element_type=jnp.float32)
    member = expert_ids[:, :, None] == jnp.arange(EXPERTS, dtype=jnp.int32)[None, None, :]
    chosen = lax.optimization_barrier(jnp.sum(jnp.where(member, jax.nn.sigmoid(logits)[:, None, :], 0.0), axis=2))
    gates = chosen / lax.optimization_barrier(jnp.sum(chosen, axis=1, keepdims=True)) * route_scale
    slot_total = N_SEQ * CAP
    flat_ids = expert_ids.reshape(-1)
    flat_gates = gates.reshape(-1)

    def one_expert(total, expert):
        flagged = flat_ids == expert
        pair_order = jnp.nonzero(flagged, size=slot_total, fill_value=0)[0].astype(jnp.int32)
        filled = jnp.arange(slot_total, dtype=jnp.int32) < jnp.sum(flagged.astype(jnp.int32))
        token_rows = pair_order // TOPK
        inputs = normed[token_rows]
        gate_part = jnp.dot(inputs, w_gate[expert], preferred_element_type=jnp.float32)
        up_part = jnp.dot(inputs, w_up[expert], preferred_element_type=jnp.float32)
        inner = (jax.nn.silu(gate_part) * up_part).astype(jnp.bfloat16).reshape(slot_total, FF // FF_PART, FF_PART)
        down_blocks = w_down[expert].reshape(FF // FF_PART, FF_PART, D)
        pieces = jnp.einsum('sbf,bfd->sbd', inner.astype(jnp.float32), down_blocks.astype(jnp.float32)).astype(jnp.bfloat16)
        pieces = lax.optimization_barrier(pieces)
        rows_out = lax.optimization_barrier(jnp.sum(pieces.astype(jnp.float32), axis=1))
        weight = jnp.where(filled, flat_gates[pair_order], 0.0)
        return (total.at[token_rows].add(rows_out * weight[:, None]), None)
    moe_total, unused = lax.scan(one_expert, jnp.zeros((TOKENS, D), jnp.float32), jnp.arange(EXPERTS, dtype=jnp.int32))
    return (attention, moe_total.astype(jnp.bfloat16))
```

```python
import math

import jax
import jax.numpy as jnp
from jax import lax
from jax.experimental import pallas as pl
from jax.experimental.pallas import tpu as pltpu
import numpy as np
from jax.sharding import PartitionSpec as P

D = 2048
NOPE = 128
ROPE = 64
VDIM = 128
LAT = 512
TOPK = 6
PRE_LEN = 512


score_scale = 1.0 / math.sqrt(192.0)
route_scale = 2.446
norm_eps = 1e-06


def request_info(lengths, group_map, position):
    request_ends = jnp.cumsum(lengths)
    request_starts = request_ends - lengths
    request_index = jnp.sum((request_ends[None, :] <= position[:, None]).astype(jnp.int32), axis=1)
    member = (
        request_index[:, None] == jnp.arange(lengths.shape[0], dtype=jnp.int32)[None, :]
    ).astype(jnp.int32)
    first_token = jnp.sum(member * request_starts[None, :], axis=1)
    token_group = jnp.sum(member * group_map[None, :], axis=1)
    return (first_token, token_group)


N_HEAD = 8
N_Z = 16
N_MATE = 4
CAP = 9
TOK = 64
COLS = D // N_HEAD
SLOTS = N_Z * N_MATE * CAP
MATE_ROWS = N_Z * CAP
Z_ROWS = N_MATE * CAP
Z_PAD = 48
PADDED = N_Z * Z_PAD
MESH = pl.DeviceIdType.MESH


def remote(src, dst, send_sem, recv_sem, device):
    return pltpu.make_async_remote_copy(
        src_ref=src,
        dst_ref=dst,
        send_sem=send_sem,
        recv_sem=recv_sem,
        device_id=device,
        device_id_type=MESH,
    )


def gather_kernel(
    prefix_ref, suffix_ref, keys_ref, local_sem, near_send, near_recv,
    seq_send, seq_recv, head_send, head_recv, core_send, core_recv,
):
    seq = lax.axis_index("seq")
    head = lax.axis_index("head")
    core = lax.rem(seq, 2)
    chip = seq // 2
    z = chip // 2
    lane = lax.rem(chip, 2)
    after = lax.rem(seq + 1, 64)
    before = lax.rem(seq + 63, 64)
    partner = seq + 1 - 2 * core

    barrier = pltpu.get_barrier_semaphore()

    def greet(n, carry):
        other = lax.rem(chip + n, 32) * 2 + core
        pl.semaphore_signal(barrier, inc=1, device_id=(other, head), device_id_type=MESH)
        return carry

    lax.fori_loop(1, 32, greet, 0)
    for n in range(1, N_HEAD):
        pl.semaphore_signal(
            barrier, inc=1, device_id=(seq, lax.rem(head + n, N_HEAD)), device_id_type=MESH
        )
    for other in (partner, after, before):
        pl.semaphore_signal(barrier, inc=1, device_id=(other, head), device_id_type=MESH)
    own_copy = pltpu.make_async_copy(suffix_ref, keys_ref.at[pl.ds(1088, 64)], local_sem.at[0])
    own_copy.start()
    pl.semaphore_wait(barrier, 31 + 7 + 3)

    near = remote(
        suffix_ref, keys_ref.at[pl.ds(1024, 64)], near_send.at[0], near_recv.at[0], (after, head)
    )
    near.start()

    base = core * 512
    group_base = base + head * 64
    mine = lax.rem(z, 8) == head
    slot = (z // 8) * 2 + lane
    place = pl.multiple_of(base + lax.rem(z, 8) * 64 + slot * 16, 16)

    def to_chip(n):
        other = lax.rem(chip + n, 32) * 2 + core
        return remote(
            prefix_ref, keys_ref.at[pl.ds(place, 16)], seq_send.at[n], seq_recv.at[slot],
            (other, head),
        )

    @pl.when(mine)
    def _():
        def send(n, carry):
            to_chip(n).start()
            return carry

        lax.fori_loop(1, 32, send, 0)
        keep = pltpu.make_async_copy(prefix_ref, keys_ref.at[pl.ds(place, 16)], local_sem.at[1])
        keep.start()
        keep.wait()

    for k in range(4):
        origin = (head + 8 * (k // 2)) * 2 + (k % 2)
        from_row = pl.multiple_of(group_base + k * 16, 16)

        @pl.when(origin != chip)
        def _():
            remote(
                prefix_ref, keys_ref.at[pl.ds(from_row, 16)], seq_send.at[0], seq_recv.at[k],
                (partner, head),
            ).wait_recv()

    def rows_of(which, owner):
        return keys_ref.at[pl.ds(pl.multiple_of(which * 512 + owner * 64, 64), 64)]

    for n in range(1, N_HEAD):
        remote(
            rows_of(core, head), rows_of(core, head), head_send.at[n], head_recv.at[head],
            (seq, lax.rem(head + n, N_HEAD)),
        ).start()
    for n in range(N_HEAD):
        owner = lax.rem(head + n, N_HEAD)
        if n:
            remote(
                rows_of(core, owner), rows_of(core, owner), head_send.at[n], head_recv.at[owner],
                (seq, owner),
            ).wait_recv()
        remote(
            rows_of(core, owner), rows_of(core, owner), core_send.at[owner], core_recv.at[owner],
            (partner, head),
        ).start()
    for owner in range(N_HEAD):
        remote(
            rows_of(core, owner), rows_of(1 - core, owner), core_send.at[owner],
            core_recv.at[owner], (partner, head),
        ).wait()

    for n in range(1, N_HEAD):
        remote(
            rows_of(core, head), rows_of(core, head), head_send.at[n], head_recv.at[head],
            (seq, lax.rem(head + n, N_HEAD)),
        ).wait_send()

    @pl.when(mine)
    def _():
        def drain(n, carry):
            to_chip(n).wait_send()
            return carry

        lax.fori_loop(1, 32, drain, 0)

    near.wait()
    own_copy.wait()


def gather_keys(prefix_latent, suffix_latent):
    dma = pltpu.SemaphoreType.DMA
    vmem = pl.BlockSpec(memory_space=pltpu.VMEM)
    return pl.pallas_call(
        gather_kernel,
        out_shape=jax.ShapeDtypeStruct((1152, LAT + ROPE), jnp.bfloat16),
        in_specs=[vmem] * 2,
        out_specs=vmem,
        scratch_shapes=[
            dma((2,)), dma((1,)), dma((1,)), dma((32,)), dma((4,)),
            dma((8,)), dma((8,)), dma((8,)), dma((8,)),
        ],
        compiler_params=pltpu.CompilerParams(collective_id=0, has_side_effects=True),
    )(prefix_latent, suffix_latent)


def slot_tables():
    slot = np.arange(SLOTS)
    mate, z, rank = slot // MATE_ROWS, slot % MATE_ROWS // CAP, slot % CAP
    expert = z * N_MATE + mate
    row = np.arange(PADDED)
    q = row % Z_PAD
    to_z = np.where(q < Z_ROWS, q // CAP * MATE_ROWS + row // Z_PAD * CAP + q % CAP, -1)
    unpad = slot + (Z_PAD - Z_ROWS) * (slot // Z_ROWS)
    return [v.astype(np.int32) for v in (expert, rank, to_z, unpad)]


def picks(column, width):
    wide = lax.broadcasted_iota(jnp.int32, (column.shape[0], width), 1)
    return jnp.where(wide == column, 1.0, 0.0).astype(jnp.bfloat16)


def picked_by(row, height):
    tall = lax.broadcasted_iota(jnp.int32, (height, row.shape[1]), 0)
    return jnp.where(tall == row, 1.0, 0.0).astype(jnp.bfloat16)


def matmul(a, b):
    return jnp.dot(a, b, preferred_element_type=jnp.float32)


def experts_kernel(
    partial_ref, residual_ref, gain_ref, router_ref, ids_ref,
    expert_col, rank_col, to_z_col, unpad_col,
    expert_row, rank_row, to_z_row, unpad_row,
    gate_ref, up_ref, down_ref,
    attention_ref, out_ref,
    sum_buf, sq_out, sq_buf, lg_out, lg_buf, slots, mates, z_out, z_in, x_buf,
    gate_acc, up_acc, inner_ref, down_out, down_in, back_out, back_in, home_out, home_in,
    sum_send, sum_recv, sq_send, sq_recv, lg_send, lg_recv, mate_send, mate_recv,
    z_send, z_recv, x_send, x_recv, down_send, down_recv, back_send, back_recv,
    home_send, home_recv,
):
    seq = lax.axis_index("seq")
    head = lax.axis_index("head")
    z = seq // N_MATE
    mate = lax.rem(seq, N_MATE)

    def head_peer(n):
        return lax.rem(head + n, N_HEAD)

    def mate_peer(n):
        return lax.rem(mate + n, N_MATE)

    def z_peer(n):
        return lax.rem(z + n, N_Z)

    barrier = pltpu.get_barrier_semaphore()

    def greet(n, carry):
        pl.semaphore_signal(
            barrier, inc=1, device_id=(z_peer(n) * N_MATE + mate, head), device_id_type=MESH
        )
        return carry

    lax.fori_loop(1, N_Z, greet, 0)
    for n in range(1, N_HEAD):
        pl.semaphore_signal(barrier, inc=1, device_id=(seq, head_peer(n)), device_id_type=MESH)
    for n in range(1, N_MATE):
        pl.semaphore_signal(
            barrier, inc=1, device_id=(z * N_MATE + mate_peer(n), head), device_id_type=MESH
        )

    lanes = lax.broadcasted_iota(jnp.int32, (TOK, 64), 1)
    member = jnp.zeros((TOK, 64), jnp.float32)
    for k in range(TOPK):
        member = member + jnp.where(ids_ref[:, k : k + 1] == lanes, 1.0, 0.0)
    below = jnp.where(lax.broadcasted_iota(jnp.int32, (TOK, 64), 0) > lanes, 1.0, 0.0)
    rank = matmul(below.astype(jnp.bfloat16), member.astype(jnp.bfloat16))
    rank = jnp.where(member > 0.5, rank, -1.0).astype(jnp.bfloat16)
    slot_rank = lax.dot_general(
        picks(expert_col[...], 64), rank, (((1,), (1,)), ((), ())),
        preferred_element_type=jnp.float32,
    )
    takes = jnp.where(slot_rank == rank_col[...].astype(jnp.float32), 1.0, 0.0).astype(jnp.bfloat16)

    pl.semaphore_wait(barrier, N_Z - 1 + N_HEAD - 1 + N_MATE - 1)

    def cols(owner):
        return pl.ds(pl.multiple_of(owner * COLS, COLS), COLS)

    def sum_copy(n):
        return remote(
            partial_ref.at[:, cols(head_peer(n))], sum_buf.at[head], sum_send.at[n],
            sum_recv.at[head], (seq, head_peer(n)),
        )

    def take(buf, send, recv, n):
        owner = head_peer(n)
        remote(buf.at[owner], buf.at[owner], send.at[n], recv.at[owner], (seq, owner)).wait_recv()

    for n in range(1, N_HEAD):
        sum_copy(n).start()
    attention = partial_ref[:, cols(head)].astype(jnp.float32)
    for n in range(1, N_HEAD):
        take(sum_buf, sum_send, sum_recv, n)
        attention = attention + sum_buf[head_peer(n)].astype(jnp.float32)
    attention_ref[...] = attention.astype(jnp.bfloat16)
    hidden = residual_ref[:, cols(head)].astype(jnp.float32) + attention
    square = jnp.sum(hidden * hidden, axis=1, keepdims=True)
    square = jnp.concatenate(
        [jnp.broadcast_to(square, (TOK, 128)), jnp.zeros((128 - TOK, 128), jnp.float32)], axis=0
    )
    square = jnp.transpose(square)[:8]
    sq_out[...] = square

    def sq_copy(n):
        return remote(
            sq_out, sq_buf.at[head], sq_send.at[n], sq_recv.at[head], (seq, head_peer(n))
        )

    for n in range(1, N_HEAD):
        sq_copy(n).start()
    for n in range(1, N_HEAD):
        take(sq_buf, sq_send, sq_recv, n)
        square = square + sq_buf[head_peer(n)]
    mean_square = jnp.transpose(jnp.broadcast_to(square[:1], (128, 128)))[:TOK, :1] * (1.0 / D)
    gain = gain_ref[:, cols(head)].astype(jnp.float32)
    normed = (hidden * lax.rsqrt(mean_square + norm_eps) * gain).astype(jnp.bfloat16)

    slots[...] = matmul(takes, normed).astype(jnp.bfloat16)

    def rows(owner):
        return pl.ds(pl.multiple_of(owner * MATE_ROWS, MATE_ROWS), MATE_ROWS)

    def mate_copy(src, dst, send, recv, n):
        owner = mate_peer(n)
        return remote(
            src.at[rows(owner)], dst.at[rows(mate)], send.at[n], recv.at[mate],
            (z * N_MATE + owner, head),
        )

    def mate_take(dst, send, recv, n):
        owner = mate_peer(n)
        remote(
            dst.at[rows(owner)], dst.at[rows(owner)], send.at[n], recv.at[owner],
            (z * N_MATE + owner, head),
        ).wait_recv()

    for n in range(1, N_MATE):
        mate_copy(slots, mates, mate_send, mate_recv, n).start()
    mates[rows(mate), :] = slots[rows(mate), :]

    lg_out[...] = matmul(normed, router_ref[cols(head), :])

    def lg_copy(n):
        return remote(
            lg_out, lg_buf.at[head], lg_send.at[n], lg_recv.at[head], (seq, head_peer(n))
        )

    for n in range(1, N_MATE):
        mate_take(mates, mate_send, mate_recv, n)
    z_out[...] = matmul(picks(to_z_col[...], SLOTS), mates[...]).astype(jnp.bfloat16)

    def z_rows(owner):
        return pl.ds(pl.multiple_of(owner * Z_PAD, Z_PAD), Z_PAD)

    def z_exchange(src, dst, send, recv):
        def copy(n):
            owner = z_peer(n)
            return remote(
                src.at[z_rows(owner)], dst.at[z_rows(z)], send.at[n], recv.at[z],
                (owner * N_MATE + mate, head),
            )

        def start(n, carry):
            copy(n).start()
            return carry

        def arrive(n, carry):
            owner = z_peer(n)
            remote(
                dst.at[z_rows(owner)], dst.at[z_rows(owner)], send.at[n], recv.at[owner],
                (owner * N_MATE + mate, head),
            ).wait_recv()
            return carry

        def drain(n, carry):
            copy(n).wait_send()
            return carry

        lax.fori_loop(1, N_Z, start, 0)
        dst[z_rows(z), :] = src[z_rows(z), :]
        return arrive, drain

    arrive, drain_z = z_exchange(z_out, z_in, z_send, z_recv)
    for n in range(1, N_HEAD):
        lg_copy(n).start()
    lax.fori_loop(1, N_Z, arrive, 0)
    x_buf[head] = matmul(picks(unpad_col[...], PADDED), z_in[...]).astype(jnp.bfloat16)

    def x_copy(n):
        return remote(
            x_buf.at[head], x_buf.at[head], x_send.at[n], x_recv.at[head], (seq, head_peer(n))
        )

    for n in range(1, N_HEAD):
        x_copy(n).start()
    gate_acc[...] = matmul(x_buf[head], gate_ref[cols(head), :])
    up_acc[...] = matmul(x_buf[head], up_ref[cols(head), :])

    def accumulate(n, carry):
        take(x_buf, x_send, x_recv, n)
        owner = head_peer(n)
        gate_acc[...] += matmul(x_buf[owner], gate_ref[cols(owner), :])
        up_acc[...] += matmul(x_buf[owner], up_ref[cols(owner), :])
        return carry

    lax.fori_loop(1, N_HEAD, accumulate, 0)
    gate = gate_acc[...]
    inner_ref[...] = (gate / (1.0 + jnp.exp(-gate)) * up_acc[...]).astype(jnp.bfloat16)

    def down_copy(n):
        owner = head_peer(n)
        return remote(
            down_out.at[owner], down_in.at[head], down_send.at[n], down_recv.at[head], (seq, owner)
        )

    def project(n, carry):
        owner = head_peer(n)
        down_out[owner] = matmul(inner_ref[...], down_ref[:, cols(owner)]).astype(jnp.bfloat16)
        down_copy(n).start()
        return carry

    lax.fori_loop(1, N_HEAD, project, 0)
    own_part = matmul(inner_ref[...], down_ref[:, cols(head)]).astype(jnp.bfloat16)
    gate_acc2 = own_part.astype(jnp.float32)

    logits = lg_out[...]
    for n in range(1, N_HEAD):
        take(lg_buf, lg_send, lg_recv, n)
        logits = logits + lg_buf[head_peer(n)]
    chosen = jnp.where(member > 0.5, 1.0 / (1.0 + jnp.exp(-logits)), 0.0)
    gates = chosen / jnp.sum(chosen, axis=1, keepdims=True) * route_scale
    by_expert = picked_by(expert_row[...], 64)
    gates_high = gates.astype(jnp.bfloat16)
    gates_low = (gates - gates_high.astype(jnp.float32)).astype(jnp.bfloat16)
    given = matmul(rank, by_expert) == rank_row[...].astype(jnp.float32)
    mix_high = jnp.where(given, matmul(gates_high, by_expert), 0.0).astype(jnp.bfloat16)
    mix_low = jnp.where(given, matmul(gates_low, by_expert), 0.0).astype(jnp.bfloat16)

    total = gate_acc2
    for n in range(1, N_HEAD):
        take(down_in, down_send, down_recv, n)
        total = total + down_in[head_peer(n)].astype(jnp.float32)
    summed = total.astype(jnp.bfloat16)
    back_out[...] = matmul(picked_by(unpad_row[...], PADDED), summed).astype(jnp.bfloat16)
    arrive, drain_back = z_exchange(back_out, back_in, back_send, back_recv)
    lax.fori_loop(1, N_Z, arrive, 0)
    home_out[...] = matmul(picked_by(to_z_row[...], SLOTS), back_in[...]).astype(jnp.bfloat16)
    for n in range(1, N_MATE):
        mate_copy(home_out, home_in, home_send, home_recv, n).start()
    home_in[rows(mate), :] = home_out[rows(mate), :]
    for n in range(1, N_MATE):
        mate_take(home_in, home_send, home_recv, n)
    out_ref[...] = (matmul(mix_high, home_in[...]) + matmul(mix_low, home_in[...])).astype(
        jnp.bfloat16
    )

    for n in range(1, N_HEAD):
        sum_copy(n).wait_send()
        sq_copy(n).wait_send()
        lg_copy(n).wait_send()
        x_copy(n).wait_send()
        down_copy(n).wait_send()
    for n in range(1, N_MATE):
        mate_copy(slots, mates, mate_send, mate_recv, n).wait_send()
        mate_copy(home_out, home_in, home_send, home_recv, n).wait_send()
    lax.fori_loop(1, N_Z, drain_z, 0)
    lax.fori_loop(1, N_Z, drain_back, 0)


def route_and_mix(partial, residual, norm_gain, router, expert_ids, w_gate, w_up, w_down):
    dma = pltpu.SemaphoreType.DMA
    vmem = pl.BlockSpec(memory_space=pltpu.VMEM)
    low, wide = jnp.bfloat16, jnp.float32
    hidden = w_gate.shape[1]
    tables = slot_tables()
    columns = [jnp.asarray(v[:, None]) for v in tables]
    across = [jnp.asarray(v[None, :]) for v in tables]
    out = jax.ShapeDtypeStruct((TOK, COLS), low)
    return pl.pallas_call(
        experts_kernel,
        out_shape=(out, out),
        in_specs=[vmem] * 16,
        out_specs=(vmem, vmem),
        scratch_shapes=[
            pltpu.VMEM((N_HEAD, TOK, COLS), low),
            pltpu.VMEM((8, 128), wide),
            pltpu.VMEM((N_HEAD, 8, 128), wide),
            pltpu.VMEM((TOK, 64), wide),
            pltpu.VMEM((N_HEAD, TOK, 64), wide),
            pltpu.VMEM((SLOTS, COLS), low),
            pltpu.VMEM((SLOTS, COLS), low),
            pltpu.VMEM((PADDED, COLS), low),
            pltpu.VMEM((PADDED, COLS), low),
            pltpu.VMEM((N_HEAD, SLOTS, COLS), low),
            pltpu.VMEM((SLOTS, hidden), wide),
            pltpu.VMEM((SLOTS, hidden), wide),
            pltpu.VMEM((SLOTS, hidden), low),
            pltpu.VMEM((N_HEAD, SLOTS, COLS), low),
            pltpu.VMEM((N_HEAD, SLOTS, COLS), low),
            pltpu.VMEM((PADDED, COLS), low),
            pltpu.VMEM((PADDED, COLS), low),
            pltpu.VMEM((SLOTS, COLS), low),
            pltpu.VMEM((SLOTS, COLS), low),
        ]
        + [dma((N_HEAD,))] * 6
        + [dma((N_MATE,))] * 2
        + [dma((N_Z,))] * 2
        + [dma((N_HEAD,))] * 4
        + [dma((N_Z,))] * 2
        + [dma((N_MATE,))] * 2,
        compiler_params=pltpu.CompilerParams(
            collective_id=1, has_side_effects=True, vmem_limit_bytes=48 * 1024 * 1024
        ),
    )(partial, residual, norm_gain, router, expert_ids, *columns, *across, w_gate, w_up, w_down)


def on_device(
    queries,
    suffix_latent,
    prefix_latent,
    kv_up,
    w_out,
    residual,
    norm_gain,
    router,
    w_gate,
    w_up,
    w_down,
    lengths,
    group_map,
    expert_ids,
):
    tok_count = queries.shape[0]
    head_local = kv_up.shape[0]
    seq_index = lax.axis_index("seq")
    first_row = seq_index * tok_count
    position = first_row + jnp.arange(tok_count, dtype=jnp.int32)
    first_token, token_group = request_info(lengths, group_map, position)
    query_block = queries.reshape(tok_count, head_local, NOPE + ROPE)
    absorbed = jnp.einsum(
        "thn,hln->thl",
        query_block[:, :, :NOPE],
        kv_up[:, :, :NOPE],
        preferred_element_type=jnp.float32,
    ).astype(jnp.bfloat16)
    joined = jnp.concatenate([absorbed, query_block[:, :, NOPE:]], axis=2).reshape(
        tok_count * head_local, LAT + ROPE
    )
    keys = gather_keys(prefix_latent, suffix_latent)
    column = jnp.arange(keys.shape[0], dtype=jnp.int32)
    near_pos = (first_row - tok_count + column - 2 * PRE_LEN)[None, :]
    near_seen = (near_pos >= first_token[:, None]) & (near_pos <= position[:, None])
    far_seen = (column[None, :] // 32) % 2 == token_group[:, None]
    seen = jnp.where(column[None, :] < 2 * PRE_LEN, far_seen, near_seen)
    seen = jnp.repeat(seen, head_local, axis=0)
    scores = jnp.dot(joined, keys.T, preferred_element_type=jnp.float32) * score_scale
    row_max = jnp.max(jnp.where(seen, scores, -jnp.inf), axis=1, keepdims=True)
    weights = jnp.where(seen, jnp.exp(scores - row_max), 0.0)
    total = jnp.sum(weights, axis=1, keepdims=True)
    weighted = jnp.dot(
        weights.astype(jnp.bfloat16), keys[:, :LAT], preferred_element_type=jnp.float32
    )
    mixed = (weighted / total).astype(jnp.bfloat16).reshape(tok_count, head_local, LAT)
    heads_out = jnp.einsum(
        "thl,hlv->thv", mixed, kv_up[:, :, NOPE:], preferred_element_type=jnp.float32
    ).astype(jnp.bfloat16)
    partial_value = jnp.dot(
        heads_out.reshape(tok_count, head_local * VDIM), w_out, preferred_element_type=jnp.float32
    )
    return route_and_mix(
        partial_value.astype(jnp.bfloat16),
        residual,
        norm_gain.reshape(1, D),
        router,
        expert_ids,
        w_gate[0],
        w_up[0],
        w_down[0],
    )


def solution(mesh):
    placed = (
        P("seq", "head"),
        P("seq", None),
        P("seq", None),
        P("head", None, None),
        P("head", None),
        P("seq", None),
        P(),
        P(),
        P("seq", None, "head"),
        P("seq", None, "head"),
        P("seq", "head", None),
        P(),
        P(),
        P("seq", None),
    )
    return jax.shard_map(
        on_device,
        mesh=mesh,
        in_specs=placed,
        out_specs=(P("seq", "head"), P("seq", "head")),
        check_vma=False,
    )
```
